32 devices in a mesh: fibre: 8 (over z, x), day: 4 (over y, core).
Axes of the slice: x: 2, y: 2, z: 4, core: 2. Of those that a mesh axis runs over, the one named last changes fastest.
Arguments:
- raw_strain: bfloat16 [4, 48, 1024, 512], P('day', None, 'fibre'), may hold values from -6 to 6
- gain_index: int32 [1024], P('fibre'), may hold values from 0 to 7
- dead_mask: int32 [1024], P('fibre'), may hold values 0 or 1
- gain_table: float32 [8], replicated, may hold values from 0.5 to 2
- source_index: int32 [4, 16], replicated, may hold values from 0 to 1023, as said below
Outputs:
- correlations: float32 [64, 1024, 256], P('day', 'fibre')
The draws below stay inside these ranges and needn't reach their ends.
Inputs may be any that keep to these rules, and one draw needn't show every extreme that they name: `source_index`: the 16 channels of a row are different and all lie in one aligned run of 128 channels, numbers k * 128 .. (k + 1) * 128 - 1. The first row lies in the first run and holds channel 0, the last row lies in the last run and holds the fibre's last channel; the run of each other row is drawn.
All inputs are finite; a program needn't handle non-finite values. No bound on the sum of `dead_mask` on one device may be relied on, other than what follows from the above.
Results may differ from the reference program's by a relative error of at most 0.0019.
Values may be sent and summed in bfloat16 or wider, within the bound.
A program may use at most 128 MiB of HBM per device.

```python
import math
import jax
import jax.numpy as jnp
from jax import lax

F = 256
SAMPLES = 512
CH_DEV = 128
SEG = 48
HALF = 16
BLOCKS = 4
BLOCK_SRC = 16
NGAIN = 8
SOURCES = 64
CHANNELS = 1024
DAYS = 4


def draw_raw_strain(key, part):
    shape = (DAYS, SEG, CHANNELS, SAMPLES)
    values = jnp.clip(jax.random.normal(key, shape, jnp.float32), -6.0, 6.0)
    times = jnp.arange(SAMPLES, dtype=jnp.int32)
    from_edge = jnp.minimum(times, SAMPLES - 1 - times).astype(jnp.float32)
    envelope = jnp.minimum(1.0, (8.0 / (from_edge + 1.0)) ** 2)
    marked = jnp.arange(SEG, dtype=jnp.int32) % 2 == 0
    factor = jnp.where(marked[:, None], envelope[None, :], 1.0)
    return (values * factor[None, :, None, :]).astype(jnp.bfloat16)


def draw_source_index(key, part):
    index_rows = []
    run_count = CHANNELS // CH_DEV
    for block in range(BLOCKS):
        block_key = jax.random.fold_in(key, 7 + block)
        if block == 0:
            rest = jax.random.permutation(jax.random.fold_in(block_key, 2), CH_DEV - 1)[:BLOCK_SRC - 1] + 1
            chosen = jnp.concatenate([jnp.zeros((1,), jnp.int32), rest.astype(jnp.int32)])
            owner_dev = jnp.int32(0)
        elif block == BLOCKS - 1:
            rest = jax.random.permutation(jax.random.fold_in(block_key, 2), CH_DEV - 1)[:BLOCK_SRC - 1]
            chosen = jnp.concatenate([rest.astype(jnp.int32), jnp.full((1,), CH_DEV - 1, jnp.int32)])
            owner_dev = jnp.int32(run_count - 1)
        else:
            owner_dev = jax.random.randint(jax.random.fold_in(block_key, 1), (), 0, run_count)
            chosen = jax.random.permutation(jax.random.fold_in(block_key, 2), CH_DEV)[:BLOCK_SRC].astype(jnp.int32)
        index_rows.append(owner_dev * CH_DEV + chosen)
    return jnp.stack(index_rows).astype(jnp.int32)


def place_ends(array, own_key, low, high):
    longest = array.shape.index(max(array.shape))
    spots = []
    for shift in (0, 1):
        where = [jax.random.randint(jax.random.fold_in(own_key, axis), (), 0, length) for axis, length in enumerate(array.shape)]
        where[longest] = (where[longest] + shift) % array.shape[longest]
        spots.append(tuple(where))
    return array.at[spots[0]].set(low).at[spots[1]].set(high)


def setup_inputs(seed: int = 0) -> dict:
    splits = jax.random.split(jax.random.key(seed), 6)
    return {
        "raw_strain": draw_raw_strain(jax.random.fold_in(splits[5], 71), 0),
        "gain_index": place_ends(jax.random.randint(splits[1], (CHANNELS,), 0, NGAIN), jax.random.fold_in(splits[1], 1), 0, NGAIN - 1).astype(jnp.int32),
        "dead_mask": place_ends((jax.random.randint(splits[2], (CHANNELS,), 0, 16) < 15).astype(jnp.int32), jax.random.fold_in(splits[2], 1), 0, 1),
        "gain_table": jnp.clip(jnp.exp(jax.random.uniform(splits[3], (NGAIN,), jnp.float32, math.log(0.5), math.log(2.0))), 0.5, 2.0),
        "source_index": draw_source_index(jax.random.fold_in(splits[5], 71), 0),
    }


def dft_table(length, bin_count):
    times = jnp.arange(length, dtype=jnp.int32)
    freqs = jnp.arange(bin_count, dtype=jnp.int32)
    phase = (times[:, None] * freqs[None, :] % length).astype(jnp.float32) * (2.0 * math.pi / length)
    taper = 0.5 - 0.5 * jnp.cos(times.astype(jnp.float32) * (2.0 * math.pi / length))
    table = jnp.concatenate([taper[:, None] * jnp.cos(phase), -taper[:, None] * jnp.sin(phase)], axis=1)
    return table.astype(jnp.bfloat16)

def band_table(bin_count, reach):
    first = jnp.arange(bin_count, dtype=jnp.int32)
    near_bins = (jnp.abs(first[:, None] - first[None, :]) <= reach).astype(jnp.float32)
    counts = lax.optimization_barrier(jnp.sum(near_bins, axis=0))
    return near_bins / counts[None, :]

def lag_table(length, bin_count, lag_count):
    freqs = jnp.arange(bin_count, dtype=jnp.int32)
    lag_vals = jnp.arange(lag_count, dtype=jnp.int32) - lag_count // 2
    phase = (freqs[:, None] * lag_vals[None, :] % length).astype(jnp.float32) * (2.0 * math.pi / length)
    weight = jnp.where(freqs == 0, 1.0, 2.0).astype(jnp.float32) / length
    return jnp.concatenate([weight[:, None] * jnp.cos(phase), -weight[:, None] * jnp.sin(phase)], axis=0)

def whiten_day(raw_day, channel_gain, forward, smoothing):
    calibrated = (raw_day.astype(jnp.float32) * channel_gain[None, :, None]).astype(jnp.bfloat16)
    values = calibrated.astype(jnp.float32)
    padded = jnp.pad(values, ((0, 0), (HALF, HALF), (0, 0)))
    window = jnp.zeros_like(values)
    for offset in range(2 * HALF + 1):
        window = window + padded[:, offset:offset + CHANNELS, :]
    detrended = values - window / (2 * HALF + 1)
    displacement = jnp.cumsum(detrended, axis=1).astype(jnp.bfloat16)
    spectra = jnp.dot(displacement.reshape(-1, SAMPLES), forward, preferred_element_type=jnp.float32)
    real_part = spectra[:, :F]
    imag_part = spectra[:, F:]
    power_bins = real_part * real_part + imag_part * imag_part
    smooth = jnp.dot(power_bins, smoothing, precision=lax.Precision.HIGHEST)
    inv_amp = lax.rsqrt(smooth + 1e-06)
    whitened = (spectra * jnp.concatenate([inv_amp, inv_amp], axis=1)).astype(jnp.bfloat16)
    return whitened.reshape(SEG, CHANNELS, 2 * F)

def cross_spectra(chosen, whitened):
    src_re = chosen[:, :, :F].astype(jnp.float32)
    src_im = chosen[:, :, F:].astype(jnp.float32)
    chan_re = whitened[:, :, :F].astype(jnp.float32)
    chan_im = whitened[:, :, F:].astype(jnp.float32)
    real_part = jnp.einsum('gsf,gcf->scf', src_re, chan_re) + jnp.einsum('gsf,gcf->scf', src_im, chan_im)
    imag_part = jnp.einsum('gsf,gcf->scf', src_im, chan_re) - jnp.einsum('gsf,gcf->scf', src_re, chan_im)
    return jnp.concatenate([real_part, imag_part], axis=2)

def reference(raw_strain, gain_index, dead_mask, gain_table, source_index):
    channel_gain = gain_table[gain_index.astype(jnp.int32)] * dead_mask.astype(jnp.float32)
    forward = dft_table(SAMPLES, F)
    smoothing = band_table(F, F // 4)
    inverse = lag_table(SAMPLES, F, F)
    flat_src = source_index.reshape(-1).astype(jnp.int32)

    def one_day(stacked, raw_day):
        whitened = whiten_day(raw_day, channel_gain, forward, smoothing)
        chosen = jnp.take(whitened, flat_src, axis=1)
        return (stacked + cross_spectra(chosen, whitened), None)
    initial = jnp.zeros((SOURCES, CHANNELS, 2 * F), jnp.float32)
    stacked, ignored = lax.scan(one_day, initial, raw_strain)
    lagged = jnp.einsum('scm,mj->scj', stacked, inverse, precision=lax.Precision.HIGHEST)
    return lagged * (1.0 / (SEG * DAYS))
```

```python
import math

import jax
import jax.numpy as jnp
from jax import lax
from jax.sharding import PartitionSpec as P

HALF = 16


def shift_rows(block, axis, width):
    count = lax.axis_size(axis)
    forward = [(i, i + 1) for i in range(count - 1)]
    backward = [(i + 1, i) for i in range(count - 1)]
    low = lax.ppermute(block[:, block.shape[1] - width:], axis, forward)
    high = lax.ppermute(block[:, :width], axis, backward)
    return low, high


def dft_table(length, bin_count):
    times = jnp.arange(length, dtype=jnp.int32)
    freqs = jnp.arange(bin_count, dtype=jnp.int32)
    phase = (times[:, None] * freqs[None, :] % length).astype(jnp.float32) * (
        2.0 * math.pi / length
    )
    taper = 0.5 - 0.5 * jnp.cos(times.astype(jnp.float32) * (2.0 * math.pi / length))
    table = jnp.concatenate(
        [taper[:, None] * jnp.cos(phase), -taper[:, None] * jnp.sin(phase)], axis=1
    )
    return table.astype(jnp.bfloat16)


def band_sum(power, reach):
    bins = power.shape[1]
    first = jnp.arange(bins, dtype=jnp.int32)
    near = jnp.abs(first[:, None] - first[None, :]) <= reach
    counts = jnp.sum(near.astype(jnp.float32), axis=0)
    band = near.astype(jnp.bfloat16)
    high = power.astype(jnp.bfloat16)
    low = (power - high.astype(jnp.float32)).astype(jnp.bfloat16)
    total = jnp.dot(high, band, preferred_element_type=jnp.float32)
    total = total + jnp.dot(low, band, preferred_element_type=jnp.float32)
    return total / counts[None, :]


def lag_table(length, bin_count, lag_count):
    freqs = jnp.arange(bin_count, dtype=jnp.int32)
    lag_vals = jnp.arange(lag_count, dtype=jnp.int32) - lag_count // 2
    phase = (freqs[:, None] * lag_vals[None, :] % length).astype(jnp.float32) * (
        2.0 * math.pi / length
    )
    weight = jnp.where(freqs == 0, 1.0, 2.0).astype(jnp.float32) / length
    return jnp.concatenate(
        [weight[:, None] * jnp.cos(phase), -weight[:, None] * jnp.sin(phase)], axis=0
    )


def whiten(displacement, table):
    segs, rows, length = displacement.shape
    bins = length // 2
    spectra = jnp.dot(
        displacement.reshape(-1, length), table, preferred_element_type=jnp.float32
    )
    real_part = spectra[:, :bins]
    imag_part = spectra[:, bins:]
    smooth = band_sum(real_part * real_part + imag_part * imag_part, bins // 4)
    inv_amp = lax.rsqrt(smooth + 1e-06)
    whitened = (spectra * jnp.concatenate([inv_amp, inv_amp], axis=1)).astype(jnp.bfloat16)
    return whitened.reshape(segs, rows, 2, bins)


def per_device(raw_strain, gain_index, dead_mask, gain_table, source_index):
    seg_count = raw_strain.shape[1]
    chan_count = raw_strain.shape[2]
    length = raw_strain.shape[3]
    bin_count = length // 2
    reach = HALF
    own_index = lax.axis_index("fibre")
    settings = jnp.arange(gain_table.shape[0], dtype=jnp.int32)
    onehot_gain = (gain_index[:, None] == settings[None, :]).astype(jnp.float32)
    channel_gain = jnp.sum(onehot_gain * gain_table[None, :], axis=1) * dead_mask.astype(
        jnp.float32
    )
    calibrated = (raw_strain[0].astype(jnp.float32) * channel_gain[None, :, None]).astype(
        jnp.bfloat16
    )
    low, high = shift_rows(calibrated, "fibre", reach)
    slope = (reach - jnp.arange(reach)).astype(jnp.float32)
    start_part = jnp.sum(calibrated[:, :reach].astype(jnp.float32) * slope[None, :, None], axis=1)
    start_term = lax.psum(jnp.where(own_index == 0, start_part, 0.0), "fibre")
    padded = jnp.concatenate([low, calibrated, high], axis=1)
    rows_here = jnp.arange(chan_count, dtype=jnp.int32)
    cols_here = jnp.arange(chan_count + 2 * reach, dtype=jnp.int32)
    offset = cols_here[None, :] - rows_here[:, None] - reach
    ramp = jnp.where(offset > 0, offset - reach - 1, offset + reach)
    ramp = jnp.where(jnp.abs(offset) <= reach, ramp, 0).astype(jnp.bfloat16)
    local = jnp.einsum("ck,gkt->gct", ramp, padded, preferred_element_type=jnp.float32)
    displacement = ((local + start_term[:, None, :]) * (1.0 / (2 * reach + 1))).astype(
        jnp.bfloat16
    )
    table = dft_table(length, bin_count)

    block_count, block_src = source_index.shape
    source_count = block_count * block_src
    flat = source_index.reshape(-1)
    here = flat // chan_count == own_index
    pick = jnp.where(here, flat - own_index * chan_count, -1)
    choose = (pick[:, None] == rows_here[None, :]).astype(jnp.bfloat16)
    offered = jnp.einsum("sc,gct->gst", choose, displacement, preferred_element_type=jnp.float32)
    chosen = lax.psum(offered.astype(jnp.bfloat16), "fibre")

    whitened = whiten(displacement, table)
    sources = whiten(chosen, table)
    swapped = jnp.stack([sources[:, :, 1], -sources[:, :, 0]], axis=2)

    inverse = lag_table(length, bin_count, bin_count).reshape(2, bin_count, bin_count)
    day = lax.axis_index("day")
    day_count = lax.axis_size("day")
    half_count = day_count // 2
    part = source_count // day_count
    near = [(i, i ^ 1) for i in range(day_count)]
    far = [(i, i ^ 2) for i in range(day_count)]

    def lagged(first):
        one = lax.dynamic_slice_in_dim(sources, first, half_count * part, axis=1)
        two = lax.dynamic_slice_in_dim(swapped, first, half_count * part, axis=1)
        both = jnp.stack([one, two], axis=0)
        cross = jnp.einsum(
            "igspf,gcpf->fisc", both, whitened, preferred_element_type=jnp.float32
        )
        return jnp.einsum("fisc,ifj->scj", cross, inverse, precision=lax.Precision.HIGH)

    def pair_sum(value):
        core = day % 2
        keep = lax.dynamic_slice_in_dim(value, core * part, part, axis=0)
        give = lax.dynamic_slice_in_dim(value, (1 - core) * part, part, axis=0)
        return keep + lax.ppermute(give.astype(jnp.bfloat16), "day", near).astype(jnp.float32)

    upper = day // 2
    other = pair_sum(lagged((1 - upper) * half_count * part))
    came = lax.ppermute(other.astype(jnp.bfloat16), "day", far)
    own = pair_sum(lagged(upper * half_count * part))
    return (own + came.astype(jnp.float32)) * (1.0 / (seg_count * day_count))


def solution(mesh):
    return jax.shard_map(
        per_device,
        mesh=mesh,
        in_specs=(P("day", None, "fibre", None), P("fibre"), P("fibre"), P(), P()),
        out_specs=P("day", "fibre", None),
        check_vma=False,
    )
```

```python
import math

import jax
import jax.numpy as jnp
from jax import lax
from jax.experimental import pallas as pl
from jax.experimental.pallas import tpu as pltpu
from jax.sharding import PartitionSpec as P

HALF = 16


def shift_rows(block, axis, width):
    count = lax.axis_size(axis)
    forward = [(i, i + 1) for i in range(count - 1)]
    backward = [(i + 1, i) for i in range(count - 1)]
    low = lax.ppermute(block[:, block.shape[1] - width:], axis, forward)
    high = lax.ppermute(block[:, :width], axis, backward)
    return low, high


def dft_table(length, bin_count):
    times = jnp.arange(length, dtype=jnp.int32)
    freqs = jnp.arange(bin_count, dtype=jnp.int32)
    phase = (times[:, None] * freqs[None, :] % length).astype(jnp.float32) * (
        2.0 * math.pi / length
    )
    taper = 0.5 - 0.5 * jnp.cos(times.astype(jnp.float32) * (2.0 * math.pi / length))
    table = jnp.concatenate(
        [taper[:, None] * jnp.cos(phase), -taper[:, None] * jnp.sin(phase)], axis=1
    )
    return table.astype(jnp.bfloat16)


def band_sum(power, reach):
    bins = power.shape[1]
    first = jnp.arange(bins, dtype=jnp.int32)
    near = jnp.abs(first[:, None] - first[None, :]) <= reach
    counts = jnp.sum(near.astype(jnp.float32), axis=0)
    band = near.astype(jnp.bfloat16)
    high = power.astype(jnp.bfloat16)
    low = (power - high.astype(jnp.float32)).astype(jnp.bfloat16)
    total = jnp.dot(high, band, preferred_element_type=jnp.float32)
    total = total + jnp.dot(low, band, preferred_element_type=jnp.float32)
    return total / counts[None, :]


def lag_table(length, bin_count, lag_count):
    freqs = jnp.arange(bin_count, dtype=jnp.int32)
    lag_vals = jnp.arange(lag_count, dtype=jnp.int32) - lag_count // 2
    phase = (freqs[:, None] * lag_vals[None, :] % length).astype(jnp.float32) * (
        2.0 * math.pi / length
    )
    weight = jnp.where(freqs == 0, 1.0, 2.0).astype(jnp.float32) / length
    return jnp.concatenate(
        [weight[:, None] * jnp.cos(phase), -weight[:, None] * jnp.sin(phase)], axis=0
    )


def whiten(displacement, table):
    segs, rows, length = displacement.shape
    bins = length // 2
    spectra = jnp.dot(
        displacement.reshape(-1, length), table, preferred_element_type=jnp.float32
    )
    real_part = spectra[:, :bins]
    imag_part = spectra[:, bins:]
    smooth = band_sum(real_part * real_part + imag_part * imag_part, bins // 4)
    inv_amp = lax.rsqrt(smooth + 1e-06)
    whitened = (spectra * jnp.concatenate([inv_amp, inv_amp], axis=1)).astype(jnp.bfloat16)
    return whitened.reshape(segs, rows, length)


def spread(block, axis, root):
    count = lax.axis_size(axis)
    step = count // 2
    while step:
        pairs = [(i ^ root, (i + step) ^ root) for i in range(0, count, 2 * step)]
        block = block + lax.ppermute(block, axis, pairs)
        step //= 2
    return block


def stack_kernel(src_re, src_im, chan_re, chan_im, high_ref, low_ref, out_ref, cross):
    step = pl.program_id(0)
    bins, segs, rows = src_re.shape
    total_bins = high_ref.shape[0] // 2
    out_rows = rows // 2
    contract = (((0,), (0,)), ((), ()))

    for place in range(bins):
        left = jnp.concatenate([src_re[place], src_im[place]], axis=0)
        right = jnp.concatenate([chan_re[place], chan_im[place]], axis=0)
        first = pl.multiple_of((step * bins + place) * rows, rows)
        cross[pl.ds(first, rows), :] = lax.dot_general(
            left, right, contract, preferred_element_type=jnp.float32
        )

    @pl.when(step == pl.num_programs(0) - 1)
    def _():
        def one(row, carry):
            total = None
            for half in range(2):
                part = cross[pl.ds(half * out_rows + row, total_bins, stride=rows), :]
                high = part.astype(jnp.bfloat16)
                low = (part - high.astype(jnp.float32)).astype(jnp.bfloat16)
                keep = pl.ds(half * total_bins, total_bins)
                for lhs, rhs in ((high, high_ref), (low, high_ref), (high, low_ref)):
                    term = lax.dot_general(
                        lhs, rhs[keep, :], contract, preferred_element_type=jnp.float32
                    )
                    total = term if total is None else total + term
            out_ref[row] = total
            return carry

        lax.fori_loop(0, out_rows, one, 0)


def stack_lags(sources, channels, inverse):
    length, segs, rows = sources.shape
    chans = channels.shape[2]
    lags = inverse.shape[1]
    step = 32
    steps = length // 2 // step
    high = inverse.astype(jnp.bfloat16)
    low = (inverse - high.astype(jnp.float32)).astype(jnp.bfloat16)
    whole = pl.BlockSpec((length, lags), lambda i: (0, 0))
    return pl.pallas_call(
        stack_kernel,
        grid=(steps,),
        in_specs=[
            pl.BlockSpec((step, segs, rows), lambda i: (i, 0, 0)),
            pl.BlockSpec((step, segs, rows), lambda i: (i + steps, 0, 0)),
            pl.BlockSpec((step, segs, chans), lambda i: (i, 0, 0)),
            pl.BlockSpec((step, segs, chans), lambda i: (i + steps, 0, 0)),
            whole,
            whole,
        ],
        out_specs=pl.BlockSpec((rows // 2, chans, lags), lambda i: (0, 0, 0)),
        out_shape=jax.ShapeDtypeStruct((rows // 2, chans, lags), jnp.float32),
        scratch_shapes=[pltpu.VMEM((length // 2 * rows, chans), jnp.float32)],
        compiler_params=pltpu.CompilerParams(vmem_limit_bytes=40 << 20),
        cost_estimate=pl.CostEstimate(
            flops=20_000_000_000, bytes_accessed=16_000_000, transcendentals=0
        ),
    )(sources, sources, channels, channels, high, low)


def per_device(raw_strain, gain_index, dead_mask, gain_table, source_index):
    seg_count = raw_strain.shape[1]
    chan_count = raw_strain.shape[2]
    length = raw_strain.shape[3]
    bin_count = length // 2
    reach = HALF
    own_index = lax.axis_index("fibre")
    settings = jnp.arange(gain_table.shape[0], dtype=jnp.int32)
    onehot_gain = (gain_index[:, None] == settings[None, :]).astype(jnp.float32)
    channel_gain = jnp.sum(onehot_gain * gain_table[None, :], axis=1) * dead_mask.astype(
        jnp.float32
    )
    calibrated = (raw_strain[0].astype(jnp.float32) * channel_gain[None, :, None]).astype(
        jnp.bfloat16
    )
    low, high = shift_rows(calibrated, "fibre", reach)
    slope = (reach - jnp.arange(reach)).astype(jnp.float32)
    start_part = jnp.sum(calibrated[:, :reach].astype(jnp.float32) * slope[None, :, None], axis=1)
    start_term = spread(jnp.where(own_index == 0, start_part, 0.0), "fibre", 0)
    padded = jnp.concatenate([low, calibrated, high], axis=1)
    rows_here = jnp.arange(chan_count, dtype=jnp.int32)
    cols_here = jnp.arange(chan_count + 2 * reach, dtype=jnp.int32)
    offset = cols_here[None, :] - rows_here[:, None] - reach
    ramp = jnp.where(offset > 0, offset - reach - 1, offset + reach)
    ramp = jnp.where(jnp.abs(offset) <= reach, ramp, 0).astype(jnp.bfloat16)
    local = jnp.einsum("ck,gkt->gct", ramp, padded, preferred_element_type=jnp.float32)
    displacement = ((local + start_term[:, None, :]) * (1.0 / (2 * reach + 1))).astype(
        jnp.bfloat16
    )
    table = dft_table(length, bin_count)

    block_count, block_src = source_index.shape
    source_count = block_count * block_src
    flat = source_index.reshape(-1)
    here = flat // chan_count == own_index
    pick = jnp.where(here, flat - own_index * chan_count, -1)
    choose = (pick[:, None] == rows_here[None, :]).astype(jnp.bfloat16)
    offered = jnp.einsum("sc,gct->gst", choose, displacement, preferred_element_type=jnp.float32)
    offered = offered.astype(jnp.bfloat16)
    middle = lax.psum(offered[:, block_src:-block_src], "fibre")
    fibre_count = lax.axis_size("fibre")
    pieces = []
    for begin in range(0, seg_count, seg_count // 2):
        cut = slice(begin, begin + seg_count // 2)
        first_block = spread(offered[cut, :block_src], "fibre", 0)
        last_block = spread(offered[cut, -block_src:], "fibre", fibre_count - 1)
        pieces.append((first_block, last_block))
    chosen = jnp.concatenate(
        [
            jnp.concatenate([piece[0] for piece in pieces], axis=0),
            middle,
            jnp.concatenate([piece[1] for piece in pieces], axis=0),
        ],
        axis=1,
    )

    whitened = whiten(displacement, table)
    sources = whiten(chosen, table)
    swapped = jnp.concatenate([sources[:, :, bin_count:], -sources[:, :, :bin_count]], axis=2)
    channels = jnp.transpose(whitened, (2, 0, 1))

    inverse = lag_table(length, bin_count, bin_count)
    day = lax.axis_index("day")
    day_count = lax.axis_size("day")
    half_count = day_count // 2
    part = source_count // day_count
    near = [(i, i ^ 1) for i in range(day_count)]
    far = [(i, i ^ 2) for i in range(day_count)]

    def lagged(first):
        one = lax.dynamic_slice_in_dim(sources, first, half_count * part, axis=1)
        two = lax.dynamic_slice_in_dim(swapped, first, half_count * part, axis=1)
        both = jnp.transpose(jnp.concatenate([one, two], axis=1), (2, 0, 1))
        return stack_lags(both, channels, inverse)

    def pair_sum(value):
        core = day % 2
        keep = lax.dynamic_slice_in_dim(value, core * part, part, axis=0)
        give = lax.dynamic_slice_in_dim(value, (1 - core) * part, part, axis=0)
        return keep + lax.ppermute(give.astype(jnp.bfloat16), "day", near).astype(jnp.float32)

    upper = day // 2
    other = pair_sum(lagged((1 - upper) * half_count * part))
    came = lax.ppermute(other.astype(jnp.bfloat16), "day", far)
    own = pair_sum(lagged(upper * half_count * part))
    return (own + came.astype(jnp.float32)) * (1.0 / (seg_count * day_count))


def solution(mesh):
    return jax.shard_map(
        per_device,
        mesh=mesh,
        in_specs=(P("day", None, "fibre", None), P("fibre"), P("fibre"), P(), P()),
        out_specs=P("day", "fibre", None),
        check_vma=False,
    )
```

```python
import math

import jax
import jax.numpy as jnp
from jax import lax
from jax.experimental import pallas as pl
from jax.experimental.pallas import tpu as pltpu
from jax.sharding import PartitionSpec as P

HALF = 16


def shift_rows(block, axis, width):
    count = lax.axis_size(axis)
    forward = [(i, i + 1) for i in range(count - 1)]
    backward = [(i + 1, i) for i in range(count - 1)]
    low = lax.ppermute(block[:, block.shape[1] - width:], axis, forward)
    high = lax.ppermute(block[:, :width], axis, backward)
    return low, high


def dft_table(length, bin_count):
    times = jnp.arange(length, dtype=jnp.int32)
    freqs = jnp.arange(bin_count, dtype=jnp.int32)
    phase = (times[:, None] * freqs[None, :] % length).astype(jnp.float32) * (
        2.0 * math.pi / length
    )
    taper = 0.5 - 0.5 * jnp.cos(times.astype(jnp.float32) * (2.0 * math.pi / length))
    table = jnp.concatenate(
        [taper[:, None] * jnp.cos(phase), -taper[:, None] * jnp.sin(phase)], axis=1
    )
    return table.astype(jnp.bfloat16)


def band_sum(power, reach):
    bins = power.shape[1]
    first = jnp.arange(bins, dtype=jnp.int32)
    near = jnp.abs(first[:, None] - first[None, :]) <= reach
    counts = jnp.sum(near.astype(jnp.float32), axis=0)
    band = near.astype(jnp.bfloat16)
    high = power.astype(jnp.bfloat16)
    low = (power - high.astype(jnp.float32)).astype(jnp.bfloat16)
    total = jnp.dot(high, band, preferred_element_type=jnp.float32)
    total = total + jnp.dot(low, band, preferred_element_type=jnp.float32)
    return total / counts[None, :]


def lag_table(length, bin_count, lag_count):
    freqs = jnp.arange(bin_count, dtype=jnp.int32)
    lag_vals = jnp.arange(lag_count, dtype=jnp.int32) - lag_count // 2
    phase = (freqs[:, None] * lag_vals[None, :] % length).astype(jnp.float32) * (
        2.0 * math.pi / length
    )
    weight = jnp.where(freqs == 0, 1.0, 2.0).astype(jnp.float32) / length
    return jnp.concatenate(
        [weight[:, None] * jnp.cos(phase), -weight[:, None] * jnp.sin(phase)], axis=0
    )


def whiten(displacement, table):
    segs, rows, length = displacement.shape
    bins = length // 2
    spectra = jnp.dot(
        displacement.reshape(-1, length), table, preferred_element_type=jnp.float32
    )
    real_part = spectra[:, :bins]
    imag_part = spectra[:, bins:]
    smooth = band_sum(real_part * real_part + imag_part * imag_part, bins // 4)
    inv_amp = lax.rsqrt(smooth + 1e-06)
    whitened = (spectra * jnp.concatenate([inv_amp, inv_amp], axis=1)).astype(jnp.bfloat16)
    return whitened.reshape(segs, rows, length)


def spread(block, axis, root):
    count = lax.axis_size(axis)
    step = count // 2
    while step:
        pairs = [(i ^ root, (i + step) ^ root) for i in range(0, count, 2 * step)]
        block = block + lax.ppermute(block, axis, pairs)
        step //= 2
    return block


def stack_kernel(src_re, src_im, chan_re, chan_im, high_ref, low_ref, out_ref, cross):
    step = pl.program_id(0)
    bins, segs, src_count = src_re.shape
    rows = 2 * src_count
    total_bins = high_ref.shape[0] // 2
    out_rows = rows // 2
    contract = (((0,), (0,)), ((), ()))

    for place in range(bins):
        real, imag = src_re[place], src_im[place]
        left = jnp.concatenate(
            [
                jnp.concatenate([real, imag], axis=1),
                jnp.concatenate([imag, -real], axis=1),
            ],
            axis=0,
        )
        right = jnp.concatenate([chan_re[place], chan_im[place]], axis=0)
        first = pl.multiple_of((step * bins + place) * rows, rows)
        cross[pl.ds(first, rows), :] = lax.dot_general(
            left, right, contract, preferred_element_type=jnp.float32
        )

    @pl.when(step == pl.num_programs(0) - 1)
    def _():
        def one(row, carry):
            total = None
            for half in range(2):
                part = cross[pl.ds(half * out_rows + row, total_bins, stride=rows), :]
                high = part.astype(jnp.bfloat16)
                low = (part - high.astype(jnp.float32)).astype(jnp.bfloat16)
                keep = pl.ds(half * total_bins, total_bins)
                for lhs, rhs in ((high, high_ref), (low, high_ref), (high, low_ref)):
                    term = lax.dot_general(
                        lhs, rhs[keep, :], contract, preferred_element_type=jnp.float32
                    )
                    total = term if total is None else total + term
            out_ref[row] = total
            return carry

        lax.fori_loop(0, out_rows, one, 0, unroll=2)


def stack_lags(sources, channels, inverse):
    length, segs, src_count = sources.shape
    rows = 2 * src_count
    chans = channels.shape[2]
    lags = inverse.shape[1]
    step = 32
    steps = length // 2 // step
    high = inverse.astype(jnp.bfloat16)
    low = (inverse - high.astype(jnp.float32)).astype(jnp.bfloat16)
    whole = pl.BlockSpec((length, lags), lambda i: (0, 0))
    return pl.pallas_call(
        stack_kernel,
        grid=(steps,),
        in_specs=[
            pl.BlockSpec((step, segs, src_count), lambda i: (i, 0, 0)),
            pl.BlockSpec((step, segs, src_count), lambda i: (i + steps, 0, 0)),
            pl.BlockSpec((step, segs, chans), lambda i: (i, 0, 0)),
            pl.BlockSpec((step, segs, chans), lambda i: (i + steps, 0, 0)),
            whole,
            whole,
        ],
        out_specs=pl.BlockSpec((rows // 2, chans, lags), lambda i: (0, 0, 0)),
        out_shape=jax.ShapeDtypeStruct((rows // 2, chans, lags), jnp.float32),
        scratch_shapes=[pltpu.VMEM((length // 2 * rows, chans), jnp.float32)],
        compiler_params=pltpu.CompilerParams(vmem_limit_bytes=48 << 20),
        cost_estimate=pl.CostEstimate(
            flops=20_000_000_000, bytes_accessed=16_000_000, transcendentals=0
        ),
    )(sources, sources, channels, channels, high, low)


def per_device(raw_strain, gain_index, dead_mask, gain_table, source_index):
    seg_count = raw_strain.shape[1]
    chan_count = raw_strain.shape[2]
    length = raw_strain.shape[3]
    bin_count = length // 2
    reach = HALF
    own_index = lax.axis_index("fibre")
    settings = jnp.arange(gain_table.shape[0], dtype=jnp.int32)
    onehot_gain = (gain_index[:, None] == settings[None, :]).astype(jnp.float32)
    channel_gain = jnp.sum(onehot_gain * gain_table[None, :], axis=1) * dead_mask.astype(
        jnp.float32
    )
    calibrated = (raw_strain[0].astype(jnp.float32) * channel_gain[None, :, None]).astype(
        jnp.bfloat16
    )
    low, high = shift_rows(calibrated, "fibre", reach)
    slope = (reach - jnp.arange(reach)).astype(jnp.float32)
    start_part = jnp.sum(calibrated[:, :reach].astype(jnp.float32) * slope[None, :, None], axis=1)
    start_term = spread(jnp.where(own_index == 0, start_part, 0.0), "fibre", 0)
    padded = jnp.concatenate([low, calibrated, high], axis=1)
    rows_here = jnp.arange(chan_count, dtype=jnp.int32)
    cols_here = jnp.arange(chan_count + 2 * reach, dtype=jnp.int32)
    offset = cols_here[None, :] - rows_here[:, None] - reach
    ramp = jnp.where(offset > 0, offset - reach - 1, offset + reach)
    ramp = jnp.where(jnp.abs(offset) <= reach, ramp, 0).astype(jnp.bfloat16)
    local = jnp.einsum("ck,gkt->gct", ramp, padded, preferred_element_type=jnp.float32)
    displacement = ((local + start_term[:, None, :]) * (1.0 / (2 * reach + 1))).astype(
        jnp.bfloat16
    )
    table = dft_table(length, bin_count)

    block_count, block_src = source_index.shape
    source_count = block_count * block_src
    flat = source_index.reshape(-1)
    here = flat // chan_count == own_index
    pick = jnp.where(here, flat - own_index * chan_count, -1)
    choose = (pick[:, None] == rows_here[None, :]).astype(jnp.bfloat16)
    offered = jnp.einsum("sc,gct->gst", choose, displacement, preferred_element_type=jnp.float32)
    offered = offered.astype(jnp.bfloat16)
    middle = lax.psum(offered[:, block_src:-block_src], "fibre")
    fibre_count = lax.axis_size("fibre")
    pieces = []
    for begin in range(0, seg_count, seg_count // 2):
        cut = slice(begin, begin + seg_count // 2)
        first_block = spread(offered[cut, :block_src], "fibre", 0)
        last_block = spread(offered[cut, -block_src:], "fibre", fibre_count - 1)
        pieces.append((first_block, last_block))
    chosen = jnp.concatenate(
        [
            jnp.concatenate([piece[0] for piece in pieces], axis=0),
            middle,
            jnp.concatenate([piece[1] for piece in pieces], axis=0),
        ],
        axis=1,
    )

    whitened = whiten(displacement, table)
    sources = whiten(chosen, table)
    channels = jnp.transpose(whitened, (2, 0, 1))
    inverse = lag_table(length, bin_count, bin_count)
    day = lax.axis_index("day")
    day_count = lax.axis_size("day")
    part = source_count // day_count
    near = [(i, i ^ 1) for i in range(day_count)]
    far = [(i, i ^ 2) for i in range(day_count)]

    lags = stack_lags(jnp.transpose(sources, (2, 0, 1)), channels, inverse)
    lags = lags.reshape(day_count // 2, 2, part, chan_count, -1)

    def pair_sum(value, place, axis, pairs):
        keep = lax.dynamic_index_in_dim(value, place, axis, False)
        give = lax.dynamic_index_in_dim(value, 1 - place, axis, False)
        came = lax.ppermute(give.astype(jnp.bfloat16), "day", pairs)
        return keep + came.astype(jnp.float32)

    total = pair_sum(pair_sum(lags, day % 2, 1, near), day // 2, 0, far)
    return total * (1.0 / (seg_count * day_count))


def solution(mesh):
    return jax.shard_map(
        per_device,
        mesh=mesh,
        in_specs=(P("day", None, "fibre", None), P("fibre"), P("fibre"), P(), P()),
        out_specs=P("day", "fibre", None),
        check_vma=False,
    )
```

```python
import math

import jax
import jax.numpy as jnp
from jax import lax
from jax.experimental import pallas as pl
from jax.experimental.pallas import tpu as pltpu
from jax.sharding import PartitionSpec as P

HALF = 16


def shift_rows(block, axis, width):
    count = lax.axis_size(axis)
    forward = [(i, i + 1) for i in range(count - 1)]
    backward = [(i + 1, i) for i in range(count - 1)]
    low = lax.ppermute(block[:, block.shape[1] - width:], axis, forward)
    high = lax.ppermute(block[:, :width], axis, backward)
    return low, high


def dft_table(length, bin_count):
    times = jnp.arange(length, dtype=jnp.int32)
    freqs = jnp.arange(bin_count, dtype=jnp.int32)
    phase = (times[:, None] * freqs[None, :] % length).astype(jnp.float32) * (
        2.0 * math.pi / length
    )
    taper = 0.5 - 0.5 * jnp.cos(times.astype(jnp.float32) * (2.0 * math.pi / length))
    table = jnp.concatenate(
        [taper[:, None] * jnp.cos(phase), -taper[:, None] * jnp.sin(phase)], axis=1
    )
    return table.astype(jnp.bfloat16)


def band_sum(power, reach):
    bins = power.shape[1]
    first = jnp.arange(bins, dtype=jnp.int32)
    near = jnp.abs(first[:, None] - first[None, :]) <= reach
    counts = jnp.sum(near.astype(jnp.float32), axis=0)
    band = near.astype(jnp.bfloat16)
    high = power.astype(jnp.bfloat16)
    low = (power - high.astype(jnp.float32)).astype(jnp.bfloat16)
    total = jnp.dot(high, band, preferred_element_type=jnp.float32)
    total = total + jnp.dot(low, band, preferred_element_type=jnp.float32)
    return total / counts[None, :]


def lag_table(length, bin_count, lag_count):
    freqs = jnp.arange(bin_count, dtype=jnp.int32)
    lag_vals = jnp.arange(lag_count, dtype=jnp.int32) - lag_count // 2
    phase = (freqs[:, None] * lag_vals[None, :] % length).astype(jnp.float32) * (
        2.0 * math.pi / length
    )
    weight = jnp.where(freqs == 0, 1.0, 2.0).astype(jnp.float32) / length
    return jnp.concatenate(
        [weight[:, None] * jnp.cos(phase), -weight[:, None] * jnp.sin(phase)], axis=0
    )


def whiten(displacement, table):
    segs, rows, length = displacement.shape
    bins = length // 2
    spectra = jnp.dot(
        displacement.reshape(-1, length), table, preferred_element_type=jnp.float32
    )
    real_part = spectra[:, :bins]
    imag_part = spectra[:, bins:]
    smooth = band_sum(real_part * real_part + imag_part * imag_part, bins // 4)
    inv_amp = lax.rsqrt(smooth + 1e-06)
    whitened = (spectra * jnp.concatenate([inv_amp, inv_amp], axis=1)).astype(jnp.bfloat16)
    return whitened.reshape(segs, rows, length)


def spread(block, axis, root):
    count = lax.axis_size(axis)
    step = count // 2
    while step:
        pairs = [(i ^ root, (i + step) ^ root) for i in range(0, count, 2 * step)]
        block = block + lax.ppermute(block, axis, pairs)
        step //= 2
    return block


def stack_kernel(end_re, end_im, mid_re, mid_im, chan_re, chan_im, high_ref, low_ref, out_ref, cross):
    step = pl.program_id(0)
    bins, segs, end_count = end_re.shape
    src_count = end_count + mid_re.shape[2]
    block = end_count // 2
    rows = 2 * src_count
    total_bins = high_ref.shape[0] // 2
    out_rows = rows // 2
    contract = (((0,), (0,)), ((), ()))

    for place in range(bins):
        real = jnp.concatenate([end_re[place], mid_re[place]], axis=1)
        imag = jnp.concatenate([end_im[place], mid_im[place]], axis=1)
        left = jnp.concatenate(
            [
                jnp.concatenate([real, imag], axis=1),
                jnp.concatenate([imag, -real], axis=1),
            ],
            axis=0,
        )
        right = jnp.concatenate([chan_re[place], chan_im[place]], axis=0)
        first = pl.multiple_of((step * bins + place) * rows, rows)
        cross[pl.ds(first, rows), :] = lax.dot_general(
            left, right, contract, preferred_element_type=jnp.float32
        )

    @pl.when(step == pl.num_programs(0) - 1)
    def _():
        def one(row, carry):
            total = None
            for half in range(2):
                part = cross[pl.ds(half * out_rows + row, total_bins, stride=rows), :]
                high = part.astype(jnp.bfloat16)
                low = (part - high.astype(jnp.float32)).astype(jnp.bfloat16)
                keep = pl.ds(half * total_bins, total_bins)
                for lhs, rhs in ((high, high_ref), (low, high_ref), (high, low_ref)):
                    term = lax.dot_general(
                        lhs, rhs[keep, :], contract, preferred_element_type=jnp.float32
                    )
                    total = term if total is None else total + term
            late = jnp.where(row < end_count, row + src_count - end_count, row - block)
            out_ref[jnp.where(row < block, row, late)] = total
            return carry

        lax.fori_loop(0, out_rows, one, 0, unroll=2)


def stack_lags(ends, middle, channels, inverse):
    length, segs, end_count = ends.shape
    mid_count = middle.shape[2]
    rows = 2 * (end_count + mid_count)
    chans = channels.shape[2]
    lags = inverse.shape[1]
    step = 32
    steps = length // 2 // step
    high = inverse.astype(jnp.bfloat16)
    low = (inverse - high.astype(jnp.float32)).astype(jnp.bfloat16)
    whole = pl.BlockSpec((length, lags), lambda i: (0, 0))
    return pl.pallas_call(
        stack_kernel,
        grid=(steps,),
        in_specs=[
            pl.BlockSpec((step, segs, end_count), lambda i: (i, 0, 0)),
            pl.BlockSpec((step, segs, end_count), lambda i: (i + steps, 0, 0)),
            pl.BlockSpec((step, segs, mid_count), lambda i: (i, 0, 0)),
            pl.BlockSpec((step, segs, mid_count), lambda i: (i + steps, 0, 0)),
            pl.BlockSpec((step, segs, chans), lambda i: (i, 0, 0)),
            pl.BlockSpec((step, segs, chans), lambda i: (i + steps, 0, 0)),
            whole,
            whole,
        ],
        out_specs=pl.BlockSpec((rows // 2, chans, lags), lambda i: (0, 0, 0)),
        out_shape=jax.ShapeDtypeStruct((rows // 2, chans, lags), jnp.float32),
        scratch_shapes=[pltpu.VMEM((length // 2 * rows, chans), jnp.float32)],
        compiler_params=pltpu.CompilerParams(vmem_limit_bytes=48 << 20),
        cost_estimate=pl.CostEstimate(
            flops=20_000_000_000, bytes_accessed=16_000_000, transcendentals=0
        ),
    )(ends, ends, middle, middle, channels, channels, high, low)


def per_device(raw_strain, gain_index, dead_mask, gain_table, source_index):
    seg_count = raw_strain.shape[1]
    chan_count = raw_strain.shape[2]
    length = raw_strain.shape[3]
    bin_count = length // 2
    reach = HALF
    own_index = lax.axis_index("fibre")
    settings = jnp.arange(gain_table.shape[0], dtype=jnp.int32)
    onehot_gain = (gain_index[:, None] == settings[None, :]).astype(jnp.float32)
    channel_gain = jnp.sum(onehot_gain * gain_table[None, :], axis=1) * dead_mask.astype(
        jnp.float32
    )
    calibrated = (raw_strain[0].astype(jnp.float32) * channel_gain[None, :, None]).astype(
        jnp.bfloat16
    )
    low, high = shift_rows(calibrated, "fibre", reach)
    slope = (reach - jnp.arange(reach)).astype(jnp.float32)
    start_part = jnp.sum(calibrated[:, :reach].astype(jnp.float32) * slope[None, :, None], axis=1)
    start_term = spread(jnp.where(own_index == 0, start_part, 0.0), "fibre", 0)
    padded = jnp.concatenate([low, calibrated, high], axis=1)
    rows_here = jnp.arange(chan_count, dtype=jnp.int32)
    cols_here = jnp.arange(chan_count + 2 * reach, dtype=jnp.int32)
    offset = cols_here[None, :] - rows_here[:, None] - reach
    ramp = jnp.where(offset > 0, offset - reach - 1, offset + reach)
    ramp = jnp.where(jnp.abs(offset) <= reach, ramp, 0).astype(jnp.bfloat16)
    local = jnp.einsum("ck,gkt->gct", ramp, padded, preferred_element_type=jnp.float32)
    displacement = ((local + start_term[:, None, :]) * (1.0 / (2 * reach + 1))).astype(
        jnp.bfloat16
    )
    table = dft_table(length, bin_count)

    block_count, block_src = source_index.shape
    source_count = block_count * block_src
    flat = source_index.reshape(-1)
    here = flat // chan_count == own_index
    pick = jnp.where(here, flat - own_index * chan_count, -1)
    choose = (pick[:, None] == rows_here[None, :]).astype(jnp.bfloat16)
    offered = jnp.einsum("sc,gct->gst", choose, displacement, preferred_element_type=jnp.float32)
    offered = offered.astype(jnp.bfloat16)
    middle = lax.psum(offered[:, block_src:-block_src], "fibre")
    fibre_count = lax.axis_size("fibre")
    pieces = []
    for begin in range(0, seg_count, seg_count // 2):
        cut = slice(begin, begin + seg_count // 2)
        first_block = spread(offered[cut, :block_src], "fibre", 0)
        last_block = spread(offered[cut, -block_src:], "fibre", fibre_count - 1)
        pieces.append((first_block, last_block))
    outer = jnp.concatenate([jnp.concatenate(piece, axis=1) for piece in pieces], axis=0)

    whitened = whiten(displacement, table)
    ends = jnp.transpose(whiten(outer, table), (2, 0, 1))
    inner = jnp.transpose(whiten(middle, table), (2, 0, 1))
    channels = jnp.transpose(whitened, (2, 0, 1))
    inverse = lag_table(length, bin_count, bin_count)
    day = lax.axis_index("day")
    day_count = lax.axis_size("day")
    part = source_count // day_count
    near = [(i, i ^ 1) for i in range(day_count)]
    far = [(i, i ^ 2) for i in range(day_count)]

    lags = stack_lags(ends, inner, channels, inverse)
    lags = lags.reshape(day_count // 2, 2, part, chan_count, -1)

    def pair_sum(value, place, axis, pairs):
        keep = lax.dynamic_index_in_dim(value, place, axis, False)
        give = lax.dynamic_index_in_dim(value, 1 - place, axis, False)
        came = lax.ppermute(give.astype(jnp.bfloat16), "day", pairs)
        return keep + came.astype(jnp.float32)

    total = pair_sum(pair_sum(lags, day % 2, 1, near), day // 2, 0, far)
    return total * (1.0 / (seg_count * day_count))


def solution(mesh):
    return jax.shard_map(
        per_device,
        mesh=mesh,
        in_specs=(P("day", None, "fibre", None), P("fibre"), P("fibre"), P(), P()),
        out_specs=P("day", "fibre", None),
        check_vma=False,
    )
```
